32 devices in a mesh: section: 2 (over y), dp: 4 (over x, core), tensor: 4 (over z).
Axes of the slice: x: 2, y: 2, z: 4, core: 2. Of those that a mesh axis runs over, the one named last changes fastest.
Arguments:
- master_weight: float32 [2304, 128, 128], P(('section', 'tensor'), 'dp'), parts along dimension 0, may hold values from -6 to 6
- first_moment: float32 [2304, 128, 128], P(('section', 'tensor'), 'dp'), parts along dimension 0, may hold values from -2 to 2
- second_moment: float32 [2304, 128, 128], P(('section', 'tensor'), 'dp'), parts along dimension 0, may hold values from 0.01 to 1
- grads: bfloat16 [4, 2304, 128, 128], P('dp', ('section', 'tensor')), parts along dimension 1, may hold values from -6 to 6
- dest_table: int32 [1152], replicated, may hold values from 0 to 1151, as said below
Outputs:
- weight_new: float32 [2304, 128, 128], P(('section', 'tensor'), 'dp'), parts along dimension 0
- first_new: float32 [2304, 128, 128], P(('section', 'tensor'), 'dp'), parts along dimension 0
- second_new: float32 [2304, 128, 128], P(('section', 'tensor'), 'dp'), parts along dimension 0
- weights: bfloat16 [2304, 128, 128], P(('section', 'tensor')), parts along dimension 0
The draws below stay inside these ranges and needn't reach their ends.
There are 2 independent parts, one for each index of `section`. The reference program is written for one: setup_inputs(seed, part) draws one part's arguments, and reference() takes and returns one part's arrays. A program takes and returns all parts, laid end to end along the dimension named above; an argument that names none is the same for every part. Nothing has to cross between parts.
Inputs may be any that keep to these rules, and one draw needn't show every extreme that they name: `dest_table`: A permutation. Group old slots by s // 288 and new positions by p // 288: at most 72 slots of one group have positions in one block, and some pair of group and block has exactly 72.
All inputs are finite; a program needn't handle non-finite values.
Results may differ from the reference program's by a relative error of at most 0.0023.
Values may be sent and summed in bfloat16 or wider, within the bound.
A program may use at most 128 MiB of HBM per device.

```python
import math
import jax
import jax.numpy as jnp
from jax import lax

HD = 128
STEP = 10
TILES = 1152
TPD = 288
TROWS = 128
N_DP = 4


def draw_dest_table(key, part):
    groups = TILES // TPD
    key_shift = jax.random.fold_in(key, 11)
    key_order = jax.random.fold_in(key, 23)
    shifts = jax.random.permutation(key_shift, groups).astype(jnp.int32)
    slot_ids = jnp.arange(TILES, dtype=jnp.int32)
    source = slot_ids // TPD
    within = slot_ids % TPD
    target = (shifts[source] + within // 2) % groups
    mixing = jax.random.permutation(key_order, TILES).astype(jnp.int32)
    ordered = jnp.argsort(target * TILES + mixing, stable=True)
    return jnp.argsort(ordered, stable=True).astype(jnp.int32)


def raised(drawn, stream_key, source, target, parts, factor):
    def block_of(dim):
        return (jnp.arange(drawn.shape[dim]) // (drawn.shape[dim] // parts)).reshape((-1,) + (1,) * (drawn.ndim - 1 - dim))

    one_side = jax.random.permutation(stream_key, parts)[block_of(target)]
    second = (block_of(target) + parts // 2) % parts
    return jnp.where((block_of(source) == one_side) | (block_of(source) == second), factor * drawn, drawn)


def levels(rng, shape, shards, low, high):
    loudness, own = 1.0, jax.random.fold_in(rng, 6)
    for dim, parts in shards:
        heights = jnp.exp(jax.random.uniform(jax.random.fold_in(own, dim), (parts,), jnp.float32, low / len(shards), high / len(shards)))
        loudness = loudness * jnp.repeat(heights, shape[dim] // parts).reshape([-1 if axis == dim else 1 for axis in range(len(shape))])
    return loudness


def scatter_about(key, extent, spread, limit, split=(), kind=jnp.bfloat16):
    array = jax.random.normal(key, extent, jnp.float32) * spread
    if len(split) > 0:
        array = levels(key, extent, split, -0.22, 0.18) * array
    return jnp.clip(array, min=-limit, max=limit).astype(kind)


def noise_with(key, dims, spread, most, split, heavy, kind=jnp.bfloat16):
    drawn = spread * jax.random.normal(key, dims, jnp.float32)
    if split:
        drawn = drawn * levels(key, dims, split, -0.22, 0.18)
    return jnp.clip(raised(drawn, jax.random.fold_in(key, 3), *heavy), -most, most).astype(kind)


def setup_inputs(seed: int = 0, part: int = 0) -> dict:
    splits = jax.random.split(jax.random.key(seed), 6)
    part_keys = jax.random.split(jax.random.fold_in(splits[5], part), 6)
    return {
        "master_weight": scatter_about(part_keys[0], (TILES, TROWS, HD), 1.0, 6.0, ((0, 4), (1, 4)), jnp.float32),
        "first_moment": scatter_about(part_keys[1], (TILES, TROWS, HD), 0.3, 2.0, ((0, 4), (1, 4)), jnp.float32),
        "second_moment": jnp.clip(jnp.exp(math.log(1.0) - 4.6051702 * jax.random.uniform(part_keys[2], (TILES, TROWS, HD), jnp.float32) ** levels(part_keys[2], (TILES, TROWS, HD), ((0, 4), (1, 4)), -0.2, 0.2)), 0.01, 1.0),
        "grads": noise_with(part_keys[3], (N_DP, TILES, TROWS, HD), 1.0, 6.0, ((0, 4), (1, 4)), (0, 2, 4, 2.0)),
        "dest_table": draw_dest_table(jax.random.fold_in(splits[5], 71), part),
    }


learn_rate = 0.04
decay_rate = 1.5
beta_first = 0.9
beta_second = 0.95
epsilon = 1e-08

def adam_step(weight, first, second, grad):
    first_new = beta_first * first + (1.0 - beta_first) * grad
    second_new = beta_second * second + (1.0 - beta_second) * grad * grad
    first_hat = first_new / (1.0 - beta_first ** STEP)
    second_hat = second_new / (1.0 - beta_second ** STEP)
    weight_new = weight - learn_rate * (first_hat / (jnp.sqrt(second_hat) + epsilon) + decay_rate * weight)
    return (weight_new, first_new, second_new)

def reference(master_weight, first_moment, second_moment, grads, dest_table):

    def placed(values):
        return jnp.zeros_like(values).at[dest_table].set(values)
    grad = lax.optimization_barrier(jnp.sum(grads.astype(jnp.float32), axis=0)) / grads.shape[0]
    weight_new, first_new, second_new = adam_step(placed(master_weight), placed(first_moment), placed(second_moment), grad)
    return (weight_new, first_new, second_new, weight_new.astype(jnp.bfloat16))
```

```python
import jax
import jax.numpy as jnp
from jax import lax
from jax.sharding import PartitionSpec as P

STEP = 10


learn_rate = 0.04
decay_rate = 1.5
beta_first = 0.9
beta_second = 0.95
epsilon = 1e-08


def adam_step(weight, first, second, grad):
    first_new = beta_first * first + (1.0 - beta_first) * grad
    second_new = beta_second * second + (1.0 - beta_second) * grad * grad
    first_hat = first_new / (1.0 - beta_first**STEP)
    second_hat = second_new / (1.0 - beta_second**STEP)
    weight_new = weight - learn_rate * (
        first_hat / (jnp.sqrt(second_hat) + epsilon) + decay_rate * weight
    )
    return (weight_new, first_new, second_new)


def routes(dest_table, slots, groups, capacity, rank_here):
    total = dest_table.shape[0]
    length = groups * capacity
    target = dest_table // slots
    local = dest_table % slots
    layout = target.reshape(groups, slots)
    order = jnp.arange(slots, dtype=jnp.int32)
    same = (layout[:, :, None] == layout[:, None, :]) & (order[None, :] < order[:, None])[None]
    within = jnp.sum(same.astype(jnp.int32), axis=2).reshape(total)
    source = jnp.arange(total, dtype=jnp.int32) // slots
    leaving = lax.dynamic_slice_in_dim(target * capacity + within, rank_here * slots, slots)
    places = jnp.arange(length, dtype=jnp.int32)
    outgoing = jnp.sum(jnp.where(leaving[None, :] == places[:, None], order[None, :], 0), axis=1)
    landing = jnp.where(target == rank_here, local, slots)
    incoming = jnp.sum(
        jnp.where(landing[None, :] == order[:, None], (source * capacity + within)[None, :], 0),
        axis=1,
    )
    return (outgoing, incoming)


def take(values, index):
    return values.at[index].get(mode="promise_in_bounds")


def shards(master_weight, first_moment, second_moment, grads, dest_table):
    groups = lax.axis_size("tensor")
    rank_here = lax.axis_index("tensor")
    slots = master_weight.shape[0]
    capacity = 2 * ((slots + 2 * groups - 1) // (2 * groups))
    outgoing, incoming = routes(dest_table, slots, groups, capacity, rank_here)
    replicas = lax.axis_size("dp")
    summed = lax.psum_scatter(grads[0], "dp", scatter_dimension=1, tiled=True).astype(jnp.float32)
    grad = summed / replicas

    def move(values):
        return lax.all_to_all(values, "tensor", split_axis=0, concat_axis=0, tiled=True)

    weight = move(take(master_weight, outgoing))
    first = move(take(first_moment, outgoing).astype(jnp.bfloat16))
    second = move(take(second_moment, outgoing).astype(jnp.bfloat16))
    weight_new, first_new, second_new = adam_step(
        take(weight, incoming),
        take(first, incoming).astype(jnp.float32),
        take(second, incoming).astype(jnp.float32),
        grad,
    )
    weights = lax.all_gather(weight_new.astype(jnp.bfloat16), "dp", axis=1, tiled=True)
    return (weight_new, first_new, second_new, weights)


def solution(mesh):
    placed = (
        P(("section", "tensor"), "dp", None),
        P(("section", "tensor"), "dp", None),
        P(("section", "tensor"), "dp", None),
        P("dp", ("section", "tensor"), None, None),
        P(),
    )
    return jax.shard_map(
        shards,
        mesh=mesh,
        in_specs=placed,
        out_specs=(
            P(("section", "tensor"), "dp", None),
            P(("section", "tensor"), "dp", None),
            P(("section", "tensor"), "dp", None),
            P(("section", "tensor"), None, None),
        ),
        check_vma=False,
    )
```

```python
import functools

import jax
import jax.numpy as jnp
from jax import lax
from jax.experimental import pallas as pl
from jax.experimental.pallas import tpu as pltpu
from jax.sharding import PartitionSpec as P

STEP = 10


learn_rate = 0.04
decay_rate = 1.5
beta_first = 0.9
beta_second = 0.95
epsilon = 1e-08


def adam_step(weight, first, second, grad):
    first_new = beta_first * first + (1.0 - beta_first) * grad
    second_new = beta_second * second + (1.0 - beta_second) * grad * grad
    first_hat = first_new / (1.0 - beta_first**STEP)
    second_hat = second_new / (1.0 - beta_second**STEP)
    weight_new = weight - learn_rate * (
        first_hat / (jnp.sqrt(second_hat) + epsilon) + decay_rate * weight
    )
    return (weight_new, first_new, second_new)


def routes(dest_table, slots, groups, capacity, rank_here):
    total = dest_table.shape[0]
    length = groups * capacity
    target = dest_table // slots
    local = dest_table % slots
    layout = target.reshape(groups, slots)
    order = jnp.arange(slots, dtype=jnp.int32)
    same = (layout[:, :, None] == layout[:, None, :]) & (order[None, :] < order[:, None])[None]
    within = jnp.sum(same.astype(jnp.int32), axis=2).reshape(total)
    source = jnp.arange(total, dtype=jnp.int32) // slots
    leaving = lax.dynamic_slice_in_dim(target * capacity + within, rank_here * slots, slots)
    places = jnp.arange(length, dtype=jnp.int32)
    outgoing = jnp.sum(jnp.where(leaving[None, :] == places[:, None], order[None, :], 0), axis=1)
    landing = jnp.where(target == rank_here, local, slots)
    incoming = jnp.sum(
        jnp.where(landing[None, :] == order[:, None], (source * capacity + within)[None, :], 0),
        axis=1,
    )
    return (outgoing, incoming)


ROWS = 8
MESH = pl.DeviceIdType.MESH


def exchange_kernel(
    groups, replicas, capacity, chunks,
    outgoing, incoming, weight, first, second, grads,
    weight_new, first_new, second_new, weights,
    raw, sent_weight, sent_moments, got_weight, got_moments, got_grads, fresh, rounded,
    load_sem, out_sem, own_sem, wide_send, wide_recv, grad_own, grad_send, grad_recv,
    last_own, last_send, last_recv,
):
    slots, rows = weight.shape[0], weight.shape[1]
    length = groups * capacity
    me = lax.axis_index("tensor")
    mine = lax.axis_index("dp")
    hops = sorted(range(1, groups), key=lambda k: -min(k, groups - k))
    turns = range(1, replicas)

    def band(chunk, owner=None):
        start = chunk * ROWS if owner is None else owner * rows + chunk * ROWS
        return pl.ds(start, ROWS)

    def loads(chunk):
        return [
            pltpu.make_async_copy(
                ref.at[:, band(chunk), :], raw[chunk % 2].at[k], load_sem.at[chunk % 2, k]
            )
            for k, ref in enumerate((weight, first, second))
        ]

    def wide(chunk, kind, source, target):
        sent, got = ((sent_weight, got_weight), (sent_moments, got_moments))[kind]
        pick = (chunk,) if kind == 0 else (chunk, slice(None))
        return pltpu.make_async_remote_copy(
            src_ref=sent.at[pick + (pl.ds(target * capacity, capacity),)],
            dst_ref=got[chunk].at[pick[1:] + (pl.ds(source * capacity, capacity),)],
            send_sem=wide_send.at[chunk, kind, target],
            recv_sem=wide_recv.at[chunk, kind, source],
            device_id={"tensor": target},
            device_id_type=MESH,
        )

    def own(chunk, kind):
        sent, got = ((sent_weight, got_weight), (sent_moments, got_moments))[kind]
        pick = (chunk,) if kind == 0 else (chunk, slice(None))
        here = pick + (pl.ds(me * capacity, capacity),)
        return pltpu.make_async_copy(
            sent.at[here], got[chunk].at[here[1:]], own_sem.at[chunk, kind]
        )

    def grad_copy(chunk, source, target):
        return pltpu.make_async_remote_copy(
            src_ref=grads.at[0, :, band(chunk, target), :],
            dst_ref=got_grads.at[source, chunk],
            send_sem=grad_send.at[chunk, target],
            recv_sem=grad_recv.at[chunk, source],
            device_id={"dp": target},
            device_id_type=MESH,
        )

    def grad_here(chunk):
        return pltpu.make_async_copy(
            grads.at[0, :, band(chunk, mine), :], got_grads.at[mine, chunk], grad_own.at[chunk]
        )

    def last_copy(chunk, source, target):
        return pltpu.make_async_remote_copy(
            src_ref=rounded.at[chunk],
            dst_ref=weights.at[:, band(chunk, source), :],
            send_sem=last_send.at[chunk, target],
            recv_sem=last_recv.at[chunk, source],
            device_id={"dp": target},
            device_id_type=MESH,
        )

    def last_here(chunk):
        return pltpu.make_async_copy(
            rounded.at[chunk], weights.at[:, band(chunk, mine), :], last_own.at[chunk]
        )

    def stores(chunk):
        return [
            pltpu.make_async_copy(
                fresh.at[chunk % 2, k], ref.at[:, band(chunk), :], out_sem.at[chunk % 2, k]
            )
            for k, ref in enumerate((weight_new, first_new, second_new))
        ]

    def start(copies):
        for copy in copies:
            copy.start()

    def finish(copies):
        for copy in copies:
            copy.wait()

    def partner(k):
        return lax.rem(me + k, groups)

    def peer(k):
        return lax.rem(mine + k, replicas)

    start(loads(0))
    if chunks > 1:
        start(loads(1))
    barrier = pltpu.get_barrier_semaphore()
    for k in hops:
        pl.semaphore_signal(barrier, inc=1, device_id={"tensor": partner(k)}, device_id_type=MESH)
    for k in turns:
        pl.semaphore_signal(barrier, inc=1, device_id={"dp": peer(k)}, device_id_type=MESH)
    pl.semaphore_wait(barrier, groups - 1 + replicas - 1)

    for chunk in range(chunks):
        finish(loads(chunk))

        def pack(j, carry, chunk=chunk):
            s = outgoing[j]
            sent_weight[chunk, j] = raw[chunk % 2][0, s]
            sent_moments[chunk, 0, j] = raw[chunk % 2][1, s].astype(jnp.bfloat16)
            sent_moments[chunk, 1, j] = raw[chunk % 2][2, s].astype(jnp.bfloat16)
            return carry

        lax.fori_loop(0, length, pack, 0, unroll=8)
        if chunk + 2 < chunks:
            start(loads(chunk + 2))
        for kind in (0, 1):
            start([wide(chunk, kind, me, partner(k)) for k in hops])
        for kind in (0, 1):
            own(chunk, kind).start()
        start([grad_copy(chunk, mine, peer(k)) for k in turns])
        grad_here(chunk).start()

    for chunk in range(chunks):
        grad_here(chunk).wait()
        for k in turns:
            grad_copy(chunk, peer(k), mine).wait_recv()
        for kind in (0, 1):
            own(chunk, kind).wait()
            for k in hops:
                wide(chunk, kind, partner(k), me).wait_recv()
        if chunk >= 2:
            finish(stores(chunk - 2))

        def update(p, carry, chunk=chunk):
            j = incoming[p]
            grad = got_grads[0, chunk, p].astype(jnp.float32)
            for r in range(1, replicas):
                grad = grad + got_grads[r, chunk, p].astype(jnp.float32)
            weight_here, first_here, second_here = adam_step(
                got_weight[chunk][j],
                got_moments[chunk][0, j].astype(jnp.float32),
                got_moments[chunk][1, j].astype(jnp.float32),
                grad / replicas,
            )
            rounded[chunk, p] = weight_here.astype(jnp.bfloat16)
            fresh[chunk % 2, 0, p] = weight_here
            fresh[chunk % 2, 1, p] = first_here
            fresh[chunk % 2, 2, p] = second_here
            return carry

        lax.fori_loop(0, slots, update, 0, unroll=4)
        start(stores(chunk))
        start([last_copy(chunk, mine, peer(k)) for k in turns])
        last_here(chunk).start()

    for chunk in range(chunks):
        last_here(chunk).wait()
        for k in turns:
            last_copy(chunk, peer(k), mine).wait_recv()
            last_copy(chunk, mine, peer(k)).wait_send()
            grad_copy(chunk, mine, peer(k)).wait_send()
        for kind in (0, 1):
            for k in hops:
                wide(chunk, kind, me, partner(k)).wait_send()
        if chunk >= chunks - 2:
            finish(stores(chunk))


def exchange(outgoing, incoming, weight, first, second, grads, groups, replicas, capacity):
    slots, rows, lanes = weight.shape
    chunks = rows // ROWS
    length = groups * capacity
    whole = jax.ShapeDtypeStruct(weight.shape, jnp.float32)
    anywhere = pl.BlockSpec(memory_space=pl.ANY)
    table = pl.BlockSpec(memory_space=pltpu.SMEM)
    dma = pltpu.SemaphoreType.DMA
    return pl.pallas_call(
        functools.partial(exchange_kernel, groups, replicas, capacity, chunks),
        out_shape=(whole, whole, whole, jax.ShapeDtypeStruct(grads.shape[1:], jnp.bfloat16)),
        in_specs=[table, table] + [anywhere] * 4,
        out_specs=(anywhere,) * 4,
        scratch_shapes=[
            [pltpu.VMEM((3, slots, ROWS, lanes), jnp.float32)] * 2,
            pltpu.VMEM((chunks, length, ROWS, lanes), jnp.float32),
            pltpu.VMEM((chunks, 2, length, ROWS, lanes), jnp.bfloat16),
            [pltpu.VMEM((length, ROWS, lanes), jnp.float32)] * chunks,
            [pltpu.VMEM((2, length, ROWS, lanes), jnp.bfloat16)] * chunks,
            pltpu.VMEM((replicas, chunks, slots, ROWS, lanes), jnp.bfloat16),
            pltpu.VMEM((2, 3, slots, ROWS, lanes), jnp.float32),
            pltpu.VMEM((chunks, slots, ROWS, lanes), jnp.bfloat16),
            dma((2, 3)),
            dma((2, 3)),
            dma((chunks, 2)),
            dma((chunks, 2, groups)),
            dma((chunks, 2, groups)),
            dma((chunks,)),
            dma((chunks, replicas)),
            dma((chunks, replicas)),
            dma((chunks,)),
            dma((chunks, replicas)),
            dma((chunks, replicas)),
        ],
        compiler_params=pltpu.CompilerParams(
            collective_id=0, has_side_effects=True, vmem_limit_bytes=60000 * 1024
        ),
        name="exchange",
    )(outgoing, incoming, weight, first, second, grads)


def shards(master_weight, first_moment, second_moment, grads, dest_table):
    groups = lax.axis_size("tensor")
    rank_here = lax.axis_index("tensor")
    slots = master_weight.shape[0]
    capacity = 2 * ((slots + 2 * groups - 1) // (2 * groups))
    outgoing, incoming = routes(dest_table, slots, groups, capacity, rank_here)
    replicas = lax.axis_size("dp")
    return exchange(
        outgoing, incoming, master_weight, first_moment, second_moment, grads,
        groups, replicas, capacity,
    )


def solution(mesh):
    placed = (
        P(("section", "tensor"), "dp", None),
        P(("section", "tensor"), "dp", None),
        P(("section", "tensor"), "dp", None),
        P("dp", ("section", "tensor"), None, None),
        P(),
    )
    return jax.shard_map(
        shards,
        mesh=mesh,
        in_specs=placed,
        out_specs=(
            P(("section", "tensor"), "dp", None),
            P(("section", "tensor"), "dp", None),
            P(("section", "tensor"), "dp", None),
            P(("section", "tensor"), None, None),
        ),
        check_vma=False,
    )
```

```python
import functools

import jax
import jax.numpy as jnp
from jax import lax
from jax.experimental import pallas as pl
from jax.experimental.pallas import tpu as pltpu
from jax.sharding import PartitionSpec as P

STEP = 10


learn_rate = 0.04
decay_rate = 1.5
beta_first = 0.9
beta_second = 0.95
epsilon = 1e-08


def adam_step(weight, first, second, grad):
    first_new = beta_first * first + (1.0 - beta_first) * grad
    second_new = beta_second * second + (1.0 - beta_second) * grad * grad
    first_hat = first_new / (1.0 - beta_first**STEP)
    second_hat = second_new / (1.0 - beta_second**STEP)
    weight_new = weight - learn_rate * (
        first_hat / (jnp.sqrt(second_hat) + epsilon) + decay_rate * weight
    )
    return (weight_new, first_new, second_new)


def routes(dest_table, slots, groups, capacity, rank_here):
    total = dest_table.shape[0]
    length = groups * capacity
    target = dest_table // slots
    local = dest_table % slots
    layout = target.reshape(groups, slots)
    order = jnp.arange(slots, dtype=jnp.int32)
    same = (layout[:, :, None] == layout[:, None, :]) & (order[None, :] < order[:, None])[None]
    within = jnp.sum(same.astype(jnp.int32), axis=2).reshape(total)
    source = jnp.arange(total, dtype=jnp.int32) // slots
    leaving = lax.dynamic_slice_in_dim(target * capacity + within, rank_here * slots, slots)
    places = jnp.arange(length, dtype=jnp.int32)
    outgoing = jnp.sum(jnp.where(leaving[None, :] == places[:, None], order[None, :], 0), axis=1)
    landing = jnp.where(target == rank_here, local, slots)
    incoming = jnp.sum(
        jnp.where(landing[None, :] == order[:, None], (source * capacity + within)[None, :], 0),
        axis=1,
    )
    return (outgoing, incoming)


ROWS = 8
SCALE = 8192.0
MESH = pl.DeviceIdType.MESH


def encode(weight):
    scaled = weight * SCALE
    square = scaled * scaled
    fourth = square * square
    return (scaled * jnp.abs(scaled) * square * fourth).astype(jnp.bfloat16)


def decode(code):
    wide = code.astype(jnp.float32)
    root = jnp.sqrt(jnp.sqrt(jnp.sqrt(jnp.abs(wide)))) * (1.0 / SCALE)
    return jnp.where(wide < 0.0, -root, root)


def exchange_kernel(
    groups, replicas, capacity, chunks,
    outgoing, incoming, weight, first, second, grads,
    weight_new, first_new, second_new, weights,
    raw, sent, got, got_grads, fresh, rounded,
    load_sem, out_sem, own_sem, wide_send, wide_recv, grad_own, grad_send, grad_recv,
    last_own, last_send, last_recv, relay_send,
):
    slots, rows = weight.shape[0], weight.shape[1]
    length = groups * capacity
    me = lax.axis_index("tensor")
    mine = lax.axis_index("dp")
    hops = sorted(range(1, groups), key=lambda k: -min(k, groups - k))
    turns = range(1, replicas)

    def band(chunk, owner=None):
        start = chunk * ROWS if owner is None else owner * rows + chunk * ROWS
        return pl.ds(start, ROWS)

    def loads(chunk):
        return [
            pltpu.make_async_copy(
                ref.at[:, band(chunk), :], raw[chunk % 2].at[k], load_sem.at[chunk % 2, k]
            )
            for k, ref in enumerate((weight, first, second))
        ]

    def wide(chunk, source, target):
        return pltpu.make_async_remote_copy(
            src_ref=sent.at[chunk, :, pl.ds(target * capacity, capacity)],
            dst_ref=got[chunk].at[:, pl.ds(source * capacity, capacity)],
            send_sem=wide_send.at[chunk, target],
            recv_sem=wide_recv.at[chunk, source],
            device_id={"tensor": target},
            device_id_type=MESH,
        )

    def own(chunk):
        here = pl.ds(me * capacity, capacity)
        return pltpu.make_async_copy(
            sent.at[chunk, :, here], got[chunk].at[:, here], own_sem.at[chunk]
        )

    def grad_copy(chunk, source, target):
        return pltpu.make_async_remote_copy(
            src_ref=grads.at[0, :, band(chunk, target), :],
            dst_ref=got_grads.at[source, chunk],
            send_sem=grad_send.at[chunk, target],
            recv_sem=grad_recv.at[chunk, source],
            device_id={"dp": target},
            device_id_type=MESH,
        )

    def grad_here(chunk):
        return pltpu.make_async_copy(
            grads.at[0, :, band(chunk, mine), :], got_grads.at[mine, chunk], grad_own.at[chunk]
        )

    def last_copy(chunk, source, target):
        return pltpu.make_async_remote_copy(
            src_ref=rounded.at[chunk],
            dst_ref=weights.at[:, band(chunk, source), :],
            send_sem=last_send.at[chunk, target],
            recv_sem=last_recv.at[chunk, source],
            device_id={"dp": target},
            device_id_type=MESH,
        )

    def relay(chunk, source):
        rows_there = weights.at[:, band(chunk, source), :]
        return pltpu.make_async_remote_copy(
            src_ref=rows_there,
            dst_ref=rows_there,
            send_sem=relay_send.at[chunk, source],
            recv_sem=last_recv.at[chunk, source],
            device_id={"dp": twin},
            device_id_type=MESH,
        )

    def last_here(chunk):
        return pltpu.make_async_copy(
            rounded.at[chunk], weights.at[:, band(chunk, mine), :], last_own.at[chunk]
        )

    def stores(chunk):
        return [
            pltpu.make_async_copy(
                fresh.at[chunk % 2, k], ref.at[:, band(chunk), :], out_sem.at[chunk % 2, k]
            )
            for k, ref in enumerate((weight_new, first_new, second_new))
        ]

    def start(copies):
        for copy in copies:
            copy.start()

    def finish(copies):
        for copy in copies:
            copy.wait()

    def partner(k):
        return lax.rem(me + k, groups)

    def peer(k):
        return lax.rem(mine + k, replicas)

    core = lax.rem(mine, 2)
    twin = mine + 1 - 2 * core
    across = range(1, replicas // 2)

    def far(k):
        return lax.rem(mine + 2 * k, replicas)

    def far_twin(k):
        return lax.rem(mine + 2 * k, replicas) + 1 - 2 * core

    start(loads(0))
    if chunks > 1:
        start(loads(1))
    barrier = pltpu.get_barrier_semaphore()
    for k in hops:
        pl.semaphore_signal(barrier, inc=1, device_id={"tensor": partner(k)}, device_id_type=MESH)
    for k in turns:
        pl.semaphore_signal(barrier, inc=1, device_id={"dp": peer(k)}, device_id_type=MESH)
    pl.semaphore_wait(barrier, groups - 1 + replicas - 1)

    for chunk in range(chunks):
        finish(loads(chunk))

        def pack(j, carry, chunk=chunk):
            s = outgoing[j]
            sent[chunk, 0, j] = encode(raw[chunk % 2][0, s])
            sent[chunk, 1, j] = raw[chunk % 2][1, s].astype(jnp.bfloat16)
            sent[chunk, 2, j] = raw[chunk % 2][2, s].astype(jnp.bfloat16)
            return carry

        lax.fori_loop(0, length, pack, 0, unroll=8)
        if chunk + 2 < chunks:
            start(loads(chunk + 2))
        start([wide(chunk, me, partner(k)) for k in hops])
        own(chunk).start()
        start([grad_copy(chunk, mine, peer(k)) for k in turns])
        grad_here(chunk).start()

    for chunk in range(chunks):
        grad_here(chunk).wait()
        for k in turns:
            grad_copy(chunk, peer(k), mine).wait_recv()
        own(chunk).wait()
        for k in hops:
            wide(chunk, partner(k), me).wait_recv()
        if chunk >= 2:
            finish(stores(chunk - 2))

        def update(p, carry, chunk=chunk):
            j = incoming[p]
            grad = got_grads[0, chunk, p].astype(jnp.float32)
            for r in range(1, replicas):
                grad = grad + got_grads[r, chunk, p].astype(jnp.float32)
            weight_here, first_here, second_here = adam_step(
                decode(got[chunk][0, j]),
                got[chunk][1, j].astype(jnp.float32),
                got[chunk][2, j].astype(jnp.float32),
                grad / replicas,
            )
            rounded[chunk, p] = weight_here.astype(jnp.bfloat16)
            fresh[chunk % 2, 0, p] = weight_here
            fresh[chunk % 2, 1, p] = first_here
            fresh[chunk % 2, 2, p] = second_here
            return carry

        lax.fori_loop(0, slots, update, 0, unroll=4)
        start(stores(chunk))
        start([last_copy(chunk, mine, far(k)) for k in across])
        last_copy(chunk, mine, twin).start()
        last_here(chunk).start()

    for chunk in range(chunks):
        for k in across:
            last_copy(chunk, far(k), mine).wait_recv()
            relay(chunk, far(k)).start()

    for chunk in range(chunks):
        last_here(chunk).wait()
        last_copy(chunk, twin, mine).wait_recv()
        last_copy(chunk, mine, twin).wait_send()
        for k in across:
            last_copy(chunk, mine, far(k)).wait_send()
            relay(chunk, far(k)).wait_send()
            relay(chunk, far_twin(k)).wait_recv()
        for k in turns:
            grad_copy(chunk, mine, peer(k)).wait_send()
        for k in hops:
            wide(chunk, me, partner(k)).wait_send()
        if chunk >= chunks - 2:
            finish(stores(chunk))


def exchange(outgoing, incoming, weight, first, second, grads, groups, replicas, capacity):
    slots, rows, lanes = weight.shape
    chunks = rows // ROWS
    length = groups * capacity
    whole = jax.ShapeDtypeStruct(weight.shape, jnp.float32)
    anywhere = pl.BlockSpec(memory_space=pl.ANY)
    table = pl.BlockSpec(memory_space=pltpu.SMEM)
    dma = pltpu.SemaphoreType.DMA
    return pl.pallas_call(
        functools.partial(exchange_kernel, groups, replicas, capacity, chunks),
        out_shape=(whole, whole, whole, jax.ShapeDtypeStruct(grads.shape[1:], jnp.bfloat16)),
        in_specs=[table, table] + [anywhere] * 4,
        out_specs=(anywhere,) * 4,
        scratch_shapes=[
            [pltpu.VMEM((3, slots, ROWS, lanes), jnp.float32)] * 2,
            pltpu.VMEM((chunks, 3, length, ROWS, lanes), jnp.bfloat16),
            [pltpu.VMEM((3, length, ROWS, lanes), jnp.bfloat16)] * chunks,
            pltpu.VMEM((replicas, chunks, slots, ROWS, lanes), jnp.bfloat16),
            pltpu.VMEM((2, 3, slots, ROWS, lanes), jnp.float32),
            pltpu.VMEM((chunks, slots, ROWS, lanes), jnp.bfloat16),
            dma((2, 3)),
            dma((2, 3)),
            dma((chunks,)),
            dma((chunks, groups)),
            dma((chunks, groups)),
            dma((chunks,)),
            dma((chunks, replicas)),
            dma((chunks, replicas)),
            dma((chunks,)),
            dma((chunks, replicas)),
            dma((chunks, replicas)),
            dma((chunks, replicas)),
        ],
        compiler_params=pltpu.CompilerParams(
            collective_id=0, has_side_effects=True, vmem_limit_bytes=60000 * 1024
        ),
        name="exchange",
    )(outgoing, incoming, weight, first, second, grads)


def shards(master_weight, first_moment, second_moment, grads, dest_table):
    groups = lax.axis_size("tensor")
    rank_here = lax.axis_index("tensor")
    slots = master_weight.shape[0]
    capacity = 2 * ((slots + 2 * groups - 1) // (2 * groups))
    outgoing, incoming = routes(dest_table, slots, groups, capacity, rank_here)
    replicas = lax.axis_size("dp")
    return exchange(
        outgoing, incoming, master_weight, first_moment, second_moment, grads,
        groups, replicas, capacity,
    )


def solution(mesh):
    placed = (
        P(("section", "tensor"), "dp", None),
        P(("section", "tensor"), "dp", None),
        P(("section", "tensor"), "dp", None),
        P("dp", ("section", "tensor"), None, None),
        P(),
    )
    return jax.shard_map(
        shards,
        mesh=mesh,
        in_specs=placed,
        out_specs=(
            P(("section", "tensor"), "dp", None),
            P(("section", "tensor"), "dp", None),
            P(("section", "tensor"), "dp", None),
            P(("section", "tensor"), None, None),
        ),
        check_vma=False,
    )
```

```python
import functools

import jax
import jax.numpy as jnp
from jax import lax
from jax.experimental import pallas as pl
from jax.experimental.pallas import tpu as pltpu
from jax.sharding import PartitionSpec as P

STEP = 10


learn_rate = 0.04
decay_rate = 1.5
beta_first = 0.9
beta_second = 0.95
epsilon = 1e-08


def adam_step(weight, first, second, grad):
    first_new = beta_first * first + (1.0 - beta_first) * grad
    second_new = beta_second * second + (1.0 - beta_second) * grad * grad
    first_hat = first_new / (1.0 - beta_first**STEP)
    second_hat = second_new / (1.0 - beta_second**STEP)
    weight_new = weight - learn_rate * (
        first_hat / (jnp.sqrt(second_hat) + epsilon) + decay_rate * weight
    )
    return (weight_new, first_new, second_new)


def routes(dest_table, slots, groups, capacity, rank_here):
    total = dest_table.shape[0]
    length = groups * capacity
    target = dest_table // slots
    local = dest_table % slots
    layout = target.reshape(groups, slots)
    order = jnp.arange(slots, dtype=jnp.int32)
    same = (layout[:, :, None] == layout[:, None, :]) & (order[None, :] < order[:, None])[None]
    within = jnp.sum(same.astype(jnp.int32), axis=2).reshape(total)
    source = jnp.arange(total, dtype=jnp.int32) // slots
    leaving = lax.dynamic_slice_in_dim(target * capacity + within, rank_here * slots, slots)
    places = jnp.arange(length, dtype=jnp.int32)
    outgoing = jnp.sum(jnp.where(leaving[None, :] == places[:, None], order[None, :], 0), axis=1)
    landing = jnp.where(target == rank_here, local, slots)
    incoming = jnp.sum(
        jnp.where(landing[None, :] == order[:, None], (source * capacity + within)[None, :], 0),
        axis=1,
    )
    return (outgoing, incoming)


ROWS = 8
SCALE = 8192.0
SPARE = 256 * 1024
MESH = pl.DeviceIdType.MESH


def encode(weight):
    scaled = weight * SCALE
    square = scaled * scaled
    fourth = square * square
    return (scaled * jnp.abs(scaled) * square * fourth).astype(jnp.bfloat16)


def decode(code):
    wide = code.astype(jnp.float32)
    root = jnp.sqrt(jnp.sqrt(jnp.sqrt(jnp.abs(wide)))) * (1.0 / SCALE)
    return jnp.where(wide < 0.0, -root, root)


def exchange_kernel(
    groups, replicas, capacity, chunks,
    outgoing, incoming, weight, first, second, grads,
    weight_new, first_new, second_new, weights,
    raw, sent, got, got_grads, rounded,
    load_sem, out_sem, own_sem, wide_send, wide_recv, grad_own, grad_send, grad_recv,
    last_own, last_send, last_recv, relay_send,
):
    slots, rows = weight.shape[0], weight.shape[1]
    length = groups * capacity
    me = lax.axis_index("tensor")
    mine = lax.axis_index("dp")
    hops = sorted(range(1, groups), key=lambda k: -min(k, groups - k))
    turns = range(1, replicas)

    def band(chunk, owner=None):
        start = chunk * ROWS if owner is None else owner * rows + chunk * ROWS
        return pl.ds(start, ROWS)

    def loads(chunk):
        return [
            pltpu.make_async_copy(
                ref.at[:, band(chunk), :], raw[chunk % 2].at[k], load_sem.at[chunk % 2, k]
            )
            for k, ref in enumerate((weight, first, second))
        ]

    def wide(chunk, source, target):
        return pltpu.make_async_remote_copy(
            src_ref=sent.at[chunk, :, pl.ds(target * capacity, capacity)],
            dst_ref=got[chunk].at[:, pl.ds(source * capacity, capacity)],
            send_sem=wide_send.at[chunk, target],
            recv_sem=wide_recv.at[chunk, source],
            device_id={"tensor": target},
            device_id_type=MESH,
        )

    def own(chunk):
        here = pl.ds(me * capacity, capacity)
        return pltpu.make_async_copy(
            sent.at[chunk, :, here], got[chunk].at[:, here], own_sem.at[chunk]
        )

    def grad_copy(chunk, source, target):
        return pltpu.make_async_remote_copy(
            src_ref=grads.at[0, :, band(chunk, target), :],
            dst_ref=got_grads.at[source, chunk],
            send_sem=grad_send.at[chunk, target],
            recv_sem=grad_recv.at[chunk, source],
            device_id={"dp": target},
            device_id_type=MESH,
        )

    def grad_here(chunk):
        return pltpu.make_async_copy(
            grads.at[0, :, band(chunk, mine), :], got_grads.at[mine, chunk], grad_own.at[chunk]
        )

    def last_copy(chunk, source, target):
        return pltpu.make_async_remote_copy(
            src_ref=rounded.at[chunk],
            dst_ref=weights.at[:, band(chunk, source), :],
            send_sem=last_send.at[chunk, target],
            recv_sem=last_recv.at[chunk, source],
            device_id={"dp": target},
            device_id_type=MESH,
        )

    def relay(chunk, source):
        rows_there = weights.at[:, band(chunk, source), :]
        return pltpu.make_async_remote_copy(
            src_ref=rows_there,
            dst_ref=rows_there,
            send_sem=relay_send.at[chunk, source],
            recv_sem=last_recv.at[chunk, source],
            device_id={"dp": twin},
            device_id_type=MESH,
        )

    def last_here(chunk):
        return pltpu.make_async_copy(
            rounded.at[chunk], weights.at[:, band(chunk, mine), :], last_own.at[chunk]
        )

    def stores(chunk):
        return [
            pltpu.make_async_copy(
                raw[chunk % 2].at[k], ref.at[:, band(chunk), :], out_sem.at[chunk % 2, k]
            )
            for k, ref in enumerate((weight_new, first_new, second_new))
        ]

    def start(copies):
        for copy in copies:
            copy.start()

    def finish(copies):
        for copy in copies:
            copy.wait()

    def partner(k):
        return lax.rem(me + k, groups)

    def peer(k):
        return lax.rem(mine + k, replicas)

    core = lax.rem(mine, 2)
    twin = mine + 1 - 2 * core
    across = range(1, replicas // 2)

    def far(k):
        return lax.rem(mine + 2 * k, replicas)

    def far_twin(k):
        return lax.rem(mine + 2 * k, replicas) + 1 - 2 * core

    start(loads(0))
    if chunks > 1:
        start(loads(1))
    barrier = pltpu.get_barrier_semaphore()
    for k in hops:
        pl.semaphore_signal(barrier, inc=1, device_id={"tensor": partner(k)}, device_id_type=MESH)
    for k in turns:
        pl.semaphore_signal(barrier, inc=1, device_id={"dp": peer(k)}, device_id_type=MESH)
    pl.semaphore_wait(barrier, groups - 1 + replicas - 1)

    for chunk in range(chunks):
        finish(loads(chunk))

        def pack(j, carry, chunk=chunk):
            s = outgoing[j]
            sent[chunk, 0, j] = encode(raw[chunk % 2][0, s])
            sent[chunk, 1, j] = raw[chunk % 2][1, s].astype(jnp.bfloat16)
            sent[chunk, 2, j] = raw[chunk % 2][2, s].astype(jnp.bfloat16)
            return carry

        lax.fori_loop(0, length, pack, 0, unroll=8)
        if chunk + 2 < chunks:
            start(loads(chunk + 2))
        start([wide(chunk, me, partner(k)) for k in hops])
        own(chunk).start()
        start([grad_copy(chunk, mine, peer(k)) for k in turns])
        grad_here(chunk).start()

    for chunk in range(chunks):
        grad_here(chunk).wait()
        for k in turns:
            grad_copy(chunk, peer(k), mine).wait_recv()
        own(chunk).wait()
        for k in hops:
            wide(chunk, partner(k), me).wait_recv()
        if chunk >= 2:
            finish(stores(chunk - 2))

        def update(p, carry, chunk=chunk):
            j = incoming[p]
            grad = got_grads[0, chunk, p].astype(jnp.float32)
            for r in range(1, replicas):
                grad = grad + got_grads[r, chunk, p].astype(jnp.float32)
            weight_here, first_here, second_here = adam_step(
                decode(got[chunk][0, j]),
                got[chunk][1, j].astype(jnp.float32),
                got[chunk][2, j].astype(jnp.float32),
                grad / replicas,
            )
            rounded[chunk, p] = weight_here.astype(jnp.bfloat16)
            raw[chunk % 2][0, p] = weight_here
            raw[chunk % 2][1, p] = first_here
            raw[chunk % 2][2, p] = second_here
            return carry

        lax.fori_loop(0, slots, update, 0, unroll=4)
        start(stores(chunk))
        start([last_copy(chunk, mine, far(k)) for k in across])
        last_copy(chunk, mine, twin).start()
        last_here(chunk).start()

    for chunk in range(chunks):
        for k in across:
            last_copy(chunk, far(k), mine).wait_recv()
            relay(chunk, far(k)).start()

    for chunk in range(chunks):
        last_here(chunk).wait()
        last_copy(chunk, twin, mine).wait_recv()
        last_copy(chunk, mine, twin).wait_send()
        for k in across:
            last_copy(chunk, mine, far(k)).wait_send()
            relay(chunk, far(k)).wait_send()
            relay(chunk, far_twin(k)).wait_recv()
        for k in turns:
            grad_copy(chunk, mine, peer(k)).wait_send()
        for k in hops:
            wide(chunk, me, partner(k)).wait_send()
        if chunk >= chunks - 2:
            finish(stores(chunk))


def exchange(outgoing, incoming, weight, first, second, grads, groups, replicas, capacity):
    slots, rows, lanes = weight.shape
    chunks = rows // ROWS
    length = groups * capacity
    whole = pltpu.VMEM(weight.shape, jnp.float32)
    anywhere = pl.BlockSpec(memory_space=pl.ANY)
    table = pl.BlockSpec(memory_space=pltpu.SMEM)
    dma = pltpu.SemaphoreType.DMA
    part = slots * ROWS * lanes
    scratch = part * (24 + 2 * chunks + 2 * chunks * replicas) + 12 * chunks * length * ROWS * lanes
    return pl.pallas_call(
        functools.partial(exchange_kernel, groups, replicas, capacity, chunks),
        out_shape=(whole, whole, whole, pltpu.VMEM(grads.shape[1:], jnp.bfloat16)),
        in_specs=[table, table] + [anywhere] * 4,
        out_specs=(anywhere,) * 4,
        scratch_shapes=[
            [pltpu.VMEM((3, slots, ROWS, lanes), jnp.float32)] * 2,
            pltpu.VMEM((chunks, 3, length, ROWS, lanes), jnp.bfloat16),
            [pltpu.VMEM((3, length, ROWS, lanes), jnp.bfloat16)] * chunks,
            pltpu.VMEM((replicas, chunks, slots, ROWS, lanes), jnp.bfloat16),
            pltpu.VMEM((chunks, slots, ROWS, lanes), jnp.bfloat16),
            dma((2, 3)),
            dma((2, 3)),
            dma((chunks,)),
            dma((chunks, groups)),
            dma((chunks, groups)),
            dma((chunks,)),
            dma((chunks, replicas)),
            dma((chunks, replicas)),
            dma((chunks,)),
            dma((chunks, replicas)),
            dma((chunks, replicas)),
            dma((chunks, replicas)),
        ],
        compiler_params=pltpu.CompilerParams(
            collective_id=0, has_side_effects=True, vmem_limit_bytes=scratch + SPARE
        ),
        name="exchange",
    )(outgoing, incoming, weight, first, second, grads)


def shards(master_weight, first_moment, second_moment, grads, dest_table):
    groups = lax.axis_size("tensor")
    rank_here = lax.axis_index("tensor")
    slots = master_weight.shape[0]
    capacity = 2 * ((slots + 2 * groups - 1) // (2 * groups))
    outgoing, incoming = routes(dest_table, slots, groups, capacity, rank_here)
    replicas = lax.axis_size("dp")
    return exchange(
        outgoing, incoming, master_weight, first_moment, second_moment, grads,
        groups, replicas, capacity,
    )


def solution(mesh):
    placed = (
        P(("section", "tensor"), "dp", None),
        P(("section", "tensor"), "dp", None),
        P(("section", "tensor"), "dp", None),
        P("dp", ("section", "tensor"), None, None),
        P(),
    )
    return jax.shard_map(
        shards,
        mesh=mesh,
        in_specs=placed,
        out_specs=(
            P(("section", "tensor"), "dp", None),
            P(("section", "tensor"), "dp", None),
            P(("section", "tensor"), "dp", None),
            P(("section", "tensor"), None, None),
        ),
        check_vma=False,
    )
```

```python
import functools
import math

import jax
import jax.numpy as jnp
from jax import lax
from jax.experimental import pallas as pl
from jax.experimental.pallas import tpu as pltpu
from jax.sharding import PartitionSpec as P

STEP = 10


learn_rate = 0.04
decay_rate = 1.5
beta_first = 0.9
beta_second = 0.95
epsilon = 1e-08


def adam_step(weight, first, second, grad):
    first_new = beta_first * first + (1.0 - beta_first) * grad
    second_new = beta_second * second + (1.0 - beta_second) * grad * grad
    first_hat = first_new * (1.0 / (1.0 - beta_first**STEP))
    second_hat = second_new * (1.0 / (1.0 - beta_second**STEP))
    weight_new = weight - learn_rate * (
        first_hat / (jnp.sqrt(second_hat) + epsilon) + decay_rate * weight
    )
    return (weight_new, first_new, second_new)


def routes(dest_table, slots, groups, capacity, rank_here):
    total = dest_table.shape[0]
    length = groups * capacity
    target = dest_table // slots
    local = dest_table % slots
    layout = target.reshape(groups, slots)
    order = jnp.arange(slots, dtype=jnp.int32)
    same = (layout[:, :, None] == layout[:, None, :]) & (order[None, :] < order[:, None])[None]
    within = jnp.sum(same.astype(jnp.int32), axis=2).reshape(total)
    source = jnp.arange(total, dtype=jnp.int32) // slots
    leaving = lax.dynamic_slice_in_dim(target * capacity + within, rank_here * slots, slots)
    places = jnp.arange(length, dtype=jnp.int32)
    outgoing = jnp.sum(jnp.where(leaving[None, :] == places[:, None], order[None, :], 0), axis=1)
    landing = jnp.where(target == rank_here, local, slots)
    incoming = jnp.sum(
        jnp.where(landing[None, :] == order[:, None], (source * capacity + within)[None, :], 0),
        axis=1,
    )
    return (outgoing, incoming)


ROWS = 8
SCALE = 8192.0
SPARE = 256 * 1024
PARTS = 4
MESH = pl.DeviceIdType.MESH


def encode(weight):
    scaled = weight * SCALE
    square = scaled * scaled
    fourth = square * square
    return (scaled * jnp.abs(scaled) * square * fourth).astype(jnp.bfloat16)


def decode(code):
    wide = code.astype(jnp.float32)
    root = jnp.sqrt(jnp.sqrt(jnp.sqrt(jnp.abs(wide)))) * (1.0 / SCALE)
    return jnp.where(wide < 0.0, -root, root)


def exchange_kernel(
    groups, replicas, capacity, chunks,
    outgoing, incoming, weight, first, second, grads,
    weight_new, first_new, second_new, weights,
    raw, sent, got, got_grads, rounded,
    load_sem, out_sem, own_sem, wide_send, wide_recv, grad_own, grad_send, grad_recv,
    last_own, last_send, last_recv, relay_send,
):
    slots, rows = weight.shape[0], weight.shape[1]
    parts = PARTS if slots % PARTS == 0 else 1
    me = lax.axis_index("tensor")
    mine = lax.axis_index("dp")
    hops = sorted(range(1, groups), key=lambda k: -min(k, groups - k))
    turns = range(1, replicas)

    def band(chunk, owner=None):
        start = chunk * ROWS if owner is None else owner * rows + chunk * ROWS
        return pl.ds(start, ROWS)

    def tiles(part):
        return pl.ds(part * (slots // parts), slots // parts)

    def loads(chunk):
        return [
            pltpu.make_async_copy(
                ref.at[:, band(chunk), :], raw[chunk % 2].at[k], load_sem.at[chunk % 2, k]
            )
            for k, ref in enumerate((weight, first, second))
        ]

    def wide(chunk, source, target):
        return pltpu.make_async_remote_copy(
            src_ref=sent.at[chunk, :, pl.ds(target * capacity, capacity)],
            dst_ref=got[chunk].at[:, pl.ds(source * capacity, capacity)],
            send_sem=wide_send.at[chunk, target],
            recv_sem=wide_recv.at[chunk, source],
            device_id={"tensor": target},
            device_id_type=MESH,
        )

    def own(chunk):
        here = pl.ds(me * capacity, capacity)
        return pltpu.make_async_copy(
            sent.at[chunk, :, here], got[chunk].at[:, here], own_sem.at[chunk]
        )

    def grad_copy(chunk, source, target):
        return pltpu.make_async_remote_copy(
            src_ref=grads.at[0, :, band(chunk, target), :],
            dst_ref=got_grads.at[source, chunk],
            send_sem=grad_send.at[chunk, target],
            recv_sem=grad_recv.at[chunk, source],
            device_id={"dp": target},
            device_id_type=MESH,
        )

    def grad_here(chunk):
        return pltpu.make_async_copy(
            grads.at[0, :, band(chunk, mine), :], got_grads.at[mine, chunk], grad_own.at[chunk]
        )

    def last_copy(chunk, part, source, target):
        return pltpu.make_async_remote_copy(
            src_ref=rounded.at[chunk, tiles(part)],
            dst_ref=weights.at[tiles(part), band(chunk, source), :],
            send_sem=last_send.at[chunk, part, target],
            recv_sem=last_recv.at[chunk, part, source],
            device_id={"dp": target},
            device_id_type=MESH,
        )

    def relay(chunk, part, source):
        rows_there = weights.at[tiles(part), band(chunk, source), :]
        return pltpu.make_async_remote_copy(
            src_ref=rows_there,
            dst_ref=rows_there,
            send_sem=relay_send.at[chunk, part, source],
            recv_sem=last_recv.at[chunk, part, source],
            device_id={"dp": twin},
            device_id_type=MESH,
        )

    def last_here(chunk):
        return pltpu.make_async_copy(
            rounded.at[chunk], weights.at[:, band(chunk, mine), :], last_own.at[chunk]
        )

    def stores(chunk):
        return [
            pltpu.make_async_copy(
                raw[chunk % 2].at[k], ref.at[:, band(chunk), :], out_sem.at[chunk % 2, k]
            )
            for k, ref in enumerate((weight_new, first_new, second_new))
        ]

    def start(copies):
        for copy in copies:
            copy.start()

    def finish(copies):
        for copy in copies:
            copy.wait()

    def partner(k):
        return lax.rem(me + k, groups)

    def peer(k):
        return lax.rem(mine + k, replicas)

    core = lax.rem(mine, 2)
    twin = mine + 1 - 2 * core
    across = range(1, replicas // 2)

    def far(k):
        return lax.rem(mine + 2 * k, replicas)

    def far_twin(k):
        return lax.rem(mine + 2 * k, replicas) + 1 - 2 * core

    start(loads(0))
    if chunks > 1:
        start(loads(1))
    barrier = pltpu.get_barrier_semaphore()
    for k in hops:
        pl.semaphore_signal(barrier, inc=1, device_id={"tensor": partner(k)}, device_id_type=MESH)
    for k in turns:
        pl.semaphore_signal(barrier, inc=1, device_id={"dp": peer(k)}, device_id_type=MESH)
    pl.semaphore_wait(barrier, groups - 1 + replicas - 1)

    for chunk in range(chunks):
        finish(loads(chunk))

        def pack(target, chunk=chunk):
            def one(i, carry):
                j = target * capacity + i
                s = outgoing[j]
                sent[chunk, 0, j] = encode(raw[chunk % 2][0, s])
                sent[chunk, 1, j] = raw[chunk % 2][1, s].astype(jnp.bfloat16)
                sent[chunk, 2, j] = raw[chunk % 2][2, s].astype(jnp.bfloat16)
                return carry

            lax.fori_loop(0, capacity, one, 0, unroll=math.gcd(capacity, 8))

        waiting = None
        for k in hops:
            pack(partner(k))
            if waiting is not None:
                waiting.start()
            waiting = wide(chunk, me, partner(k))
        pack(me)
        if waiting is not None:
            waiting.start()
        if chunk + 2 < chunks:
            start(loads(chunk + 2))
        own(chunk).start()
        start([grad_copy(chunk, mine, peer(k)) for k in turns])
        grad_here(chunk).start()

    for chunk in range(chunks):
        grad_here(chunk).wait()
        for k in turns:
            grad_copy(chunk, peer(k), mine).wait_recv()
        own(chunk).wait()
        for k in hops:
            wide(chunk, partner(k), me).wait_recv()
        if chunk >= 2:
            finish(stores(chunk - 2))

        def update(p, carry, chunk=chunk):
            j = incoming[p]
            grad = got_grads[0, chunk, p].astype(jnp.float32)
            for r in range(1, replicas):
                grad = grad + got_grads[r, chunk, p].astype(jnp.float32)
            weight_here, first_here, second_here = adam_step(
                decode(got[chunk][0, j]),
                got[chunk][1, j].astype(jnp.float32),
                got[chunk][2, j].astype(jnp.float32),
                grad * (1.0 / replicas),
            )
            rounded[chunk, p] = weight_here.astype(jnp.bfloat16)
            raw[chunk % 2][0, p] = weight_here
            raw[chunk % 2][1, p] = first_here
            raw[chunk % 2][2, p] = second_here
            return carry

        size = slots // parts
        for part in range(parts):
            lax.fori_loop(part * size, (part + 1) * size, update, 0, unroll=math.gcd(size, 8))
            start([last_copy(chunk, part, mine, far(k)) for k in across])
            last_copy(chunk, part, mine, twin).start()
        start(stores(chunk))
        last_here(chunk).start()

    pieces = [(chunk, part) for chunk in range(chunks) for part in range(parts)]
    for chunk, part in pieces:
        for k in across:
            last_copy(chunk, part, far(k), mine).wait_recv()
            relay(chunk, part, far(k)).start()

    for chunk, part in pieces:
        last_copy(chunk, part, twin, mine).wait_recv()
        last_copy(chunk, part, mine, twin).wait_send()
        for k in across:
            last_copy(chunk, part, mine, far(k)).wait_send()
            relay(chunk, part, far(k)).wait_send()
            relay(chunk, part, far_twin(k)).wait_recv()

    for chunk in range(chunks):
        last_here(chunk).wait()
        for k in turns:
            grad_copy(chunk, mine, peer(k)).wait_send()
        for k in hops:
            wide(chunk, me, partner(k)).wait_send()
        if chunk >= chunks - 2:
            finish(stores(chunk))


def exchange(outgoing, incoming, weight, first, second, grads, groups, replicas, capacity):
    slots, rows, lanes = weight.shape
    chunks = rows // ROWS
    length = groups * capacity
    whole = pltpu.VMEM(weight.shape, jnp.float32)
    anywhere = pl.BlockSpec(memory_space=pl.ANY)
    table = pl.BlockSpec(memory_space=pltpu.SMEM)
    dma = pltpu.SemaphoreType.DMA
    parts = PARTS if slots % PARTS == 0 else 1
    block = slots * ROWS * lanes
    scratch = block * (24 + 2 * chunks + 2 * chunks * replicas) + 12 * chunks * length * ROWS * lanes
    return pl.pallas_call(
        functools.partial(exchange_kernel, groups, replicas, capacity, chunks),
        out_shape=(whole, whole, whole, pltpu.VMEM(grads.shape[1:], jnp.bfloat16)),
        in_specs=[table, table] + [anywhere] * 4,
        out_specs=(anywhere,) * 4,
        scratch_shapes=[
            [pltpu.VMEM((3, slots, ROWS, lanes), jnp.float32)] * 2,
            pltpu.VMEM((chunks, 3, length, ROWS, lanes), jnp.bfloat16),
            [pltpu.VMEM((3, length, ROWS, lanes), jnp.bfloat16)] * chunks,
            pltpu.VMEM((replicas, chunks, slots, ROWS, lanes), jnp.bfloat16),
            pltpu.VMEM((chunks, slots, ROWS, lanes), jnp.bfloat16),
            dma((2, 3)),
            dma((2, 3)),
            dma((chunks,)),
            dma((chunks, groups)),
            dma((chunks, groups)),
            dma((chunks,)),
            dma((chunks, replicas)),
            dma((chunks, replicas)),
            dma((chunks,)),
            dma((chunks, parts, replicas)),
            dma((chunks, parts, replicas)),
            dma((chunks, parts, replicas)),
        ],
        compiler_params=pltpu.CompilerParams(
            collective_id=0, has_side_effects=True, vmem_limit_bytes=scratch + SPARE
        ),
        name="exchange",
    )(outgoing, incoming, weight, first, second, grads)


def shards(master_weight, first_moment, second_moment, grads, dest_table):
    groups = lax.axis_size("tensor")
    rank_here = lax.axis_index("tensor")
    slots = master_weight.shape[0]
    capacity = 2 * ((slots + 2 * groups - 1) // (2 * groups))
    outgoing, incoming = routes(dest_table, slots, groups, capacity, rank_here)
    replicas = lax.axis_size("dp")
    return exchange(
        outgoing, incoming, master_weight, first_moment, second_moment, grads,
        groups, replicas, capacity,
    )


def solution(mesh):
    placed = (
        P(("section", "tensor"), "dp", None),
        P(("section", "tensor"), "dp", None),
        P(("section", "tensor"), "dp", None),
        P("dp", ("section", "tensor"), None, None),
        P(),
    )
    return jax.shard_map(
        shards,
        mesh=mesh,
        in_specs=placed,
        out_specs=(
            P(("section", "tensor"), "dp", None),
            P(("section", "tensor"), "dp", None),
            P(("section", "tensor"), "dp", None),
            P(("section", "tensor"), None, None),
        ),
        check_vma=False,
    )
```

```python
import functools
import math

import jax
import jax.numpy as jnp
from jax import lax
from jax.experimental import pallas as pl
from jax.experimental.pallas import tpu as pltpu
from jax.sharding import PartitionSpec as P

STEP = 10


learn_rate = 0.04
decay_rate = 1.5
beta_first = 0.9
beta_second = 0.95
epsilon = 1e-08


def adam_step(weight, first, second, grad):
    first_new = beta_first * first + (1.0 - beta_first) * grad
    second_new = beta_second * second + (1.0 - beta_second) * grad * grad
    first_hat = first_new * (1.0 / (1.0 - beta_first**STEP))
    second_hat = second_new * (1.0 / (1.0 - beta_second**STEP))
    weight_new = weight - learn_rate * (
        first_hat / (jnp.sqrt(second_hat) + epsilon) + decay_rate * weight
    )
    return (weight_new, first_new, second_new)


def routes(dest_table, slots, groups, capacity, rank_here):
    total = dest_table.shape[0]
    length = groups * capacity
    target = dest_table // slots
    local = dest_table % slots
    layout = target.reshape(groups, slots)
    order = jnp.arange(slots, dtype=jnp.int32)
    same = (layout[:, :, None] == layout[:, None, :]) & (order[None, :] < order[:, None])[None]
    within = jnp.sum(same.astype(jnp.int32), axis=2).reshape(total)
    source = jnp.arange(total, dtype=jnp.int32) // slots
    leaving = lax.dynamic_slice_in_dim(target * capacity + within, rank_here * slots, slots)
    places = jnp.arange(length, dtype=jnp.int32)
    outgoing = jnp.sum(jnp.where(leaving[None, :] == places[:, None], order[None, :], 0), axis=1)
    landing = jnp.where(target == rank_here, local, slots)
    incoming = jnp.sum(
        jnp.where(landing[None, :] == order[:, None], (source * capacity + within)[None, :], 0),
        axis=1,
    )
    return (outgoing, incoming)


ROWS = 8
SCALE = 8192.0
SPARE = 256 * 1024
PARTS = 4
MESH = pl.DeviceIdType.MESH


def encode(weight):
    scaled = weight * SCALE
    square = scaled * scaled
    fourth = square * square
    return (scaled * jnp.abs(scaled) * square * fourth).astype(jnp.bfloat16)


def decode(code):
    wide = code.astype(jnp.float32)
    root = jnp.sqrt(jnp.sqrt(jnp.sqrt(jnp.abs(wide)))) * (1.0 / SCALE)
    return jnp.where(wide < 0.0, -root, root)


def exchange_kernel(
    groups, replicas, capacity, chunks,
    outgoing, incoming, weight, first, second, grads,
    weight_new, first_new, second_new, weights,
    raw, sent, got, got_grads, rounded,
    load_sem, out_sem, own_sem, wide_send, wide_recv, grad_own, grad_send, grad_recv,
    last_own, last_send, last_recv, relay_send,
):
    slots, rows = weight.shape[0], weight.shape[1]
    parts = PARTS if slots % PARTS == 0 else 1
    me = lax.axis_index("tensor")
    mine = lax.axis_index("dp")
    hops = range(1, groups)
    turns = range(1, replicas)

    def band(chunk, owner=None):
        start = chunk * ROWS if owner is None else owner * rows + chunk * ROWS
        return pl.ds(start, ROWS)

    def tiles(part):
        return pl.ds(part * (slots // parts), slots // parts)

    def loads(chunk):
        return [
            pltpu.make_async_copy(
                ref.at[:, band(chunk), :], raw[chunk % 2].at[k], load_sem.at[chunk % 2, k]
            )
            for k, ref in enumerate((weight, first, second))
        ]

    def wide(chunk, source, target):
        return pltpu.make_async_remote_copy(
            src_ref=sent.at[chunk, :, pl.ds(target * capacity, capacity)],
            dst_ref=got[chunk].at[:, pl.ds(source * capacity, capacity)],
            send_sem=wide_send.at[chunk, target],
            recv_sem=wide_recv.at[chunk, source],
            device_id={"tensor": target},
            device_id_type=MESH,
        )

    def own(chunk):
        here = pl.ds(me * capacity, capacity)
        return pltpu.make_async_copy(
            sent.at[chunk, :, here], got[chunk].at[:, here], own_sem.at[chunk]
        )

    def grad_copy(chunk, source, target):
        return pltpu.make_async_remote_copy(
            src_ref=grads.at[0, :, band(chunk, target), :],
            dst_ref=got_grads.at[source, chunk],
            send_sem=grad_send.at[chunk, target],
            recv_sem=grad_recv.at[chunk, source],
            device_id={"dp": target},
            device_id_type=MESH,
        )

    def grad_here(chunk):
        return pltpu.make_async_copy(
            grads.at[0, :, band(chunk, mine), :], got_grads.at[mine, chunk], grad_own.at[chunk]
        )

    def last_copy(chunk, part, source, target):
        return pltpu.make_async_remote_copy(
            src_ref=rounded.at[chunk, tiles(part)],
            dst_ref=weights.at[tiles(part), band(chunk, source), :],
            send_sem=last_send.at[chunk, part, target],
            recv_sem=last_recv.at[chunk, part, source],
            device_id={"dp": target},
            device_id_type=MESH,
        )

    def relay(chunk, part, source):
        rows_there = weights.at[tiles(part), band(chunk, source), :]
        return pltpu.make_async_remote_copy(
            src_ref=rows_there,
            dst_ref=rows_there,
            send_sem=relay_send.at[chunk, part, source],
            recv_sem=last_recv.at[chunk, part, source],
            device_id={"dp": twin},
            device_id_type=MESH,
        )

    def last_here(chunk):
        return pltpu.make_async_copy(
            rounded.at[chunk], weights.at[:, band(chunk, mine), :], last_own.at[chunk]
        )

    def stores(chunk):
        return [
            pltpu.make_async_copy(
                raw[chunk % 2].at[k], ref.at[:, band(chunk), :], out_sem.at[chunk % 2, k]
            )
            for k, ref in enumerate((weight_new, first_new, second_new))
        ]

    def start(copies):
        for copy in copies:
            copy.start()

    def finish(copies):
        for copy in copies:
            copy.wait()

    def partner(k):
        if groups & (groups - 1):
            return lax.rem(me + k, groups)
        there = me
        for bit in (1 << n for n in range(k.bit_length())):
            if k & bit:
                there = there + bit - 2 * bit * lax.rem(there // bit, 2)
        return there

    inner = (me > 0) & (me < groups - 1)

    def peer(k):
        return lax.rem(mine + k, replicas)

    core = lax.rem(mine, 2)
    twin = mine + 1 - 2 * core
    across = range(1, replicas // 2)

    def far(k):
        return lax.rem(mine + 2 * k, replicas)

    def far_twin(k):
        return lax.rem(mine + 2 * k, replicas) + 1 - 2 * core

    start(loads(0))
    if chunks > 1:
        start(loads(1))
    barrier = pltpu.get_barrier_semaphore()
    for k in hops:
        pl.semaphore_signal(barrier, inc=1, device_id={"tensor": partner(k)}, device_id_type=MESH)
    for k in turns:
        pl.semaphore_signal(barrier, inc=1, device_id={"dp": peer(k)}, device_id_type=MESH)
    pl.semaphore_wait(barrier, groups - 1 + replicas - 1)

    for chunk in range(chunks):
        finish(loads(chunk))

        def pack(target, chunk=chunk):
            def one(i, carry):
                j = target * capacity + i
                s = outgoing[j]
                sent[chunk, 0, j] = encode(raw[chunk % 2][0, s])
                sent[chunk, 1, j] = raw[chunk % 2][1, s].astype(jnp.bfloat16)
                sent[chunk, 2, j] = raw[chunk % 2][2, s].astype(jnp.bfloat16)
                return carry

            lax.fori_loop(0, capacity, one, 0, unroll=math.gcd(capacity, 8))

        def send(k, chunk=chunk):
            if k == 1:
                wide(chunk, me, partner(k)).start()
            elif k > 1:
                pl.when(inner)(lambda: wide(chunk, me, partner(k)).start())

        for k in hops:
            pack(partner(k))
            send(k - 1)
        pack(me)
        send(groups - 1)
        if chunk + 2 < chunks:
            start(loads(chunk + 2))
        own(chunk).start()
        start([grad_copy(chunk, mine, peer(k)) for k in turns])
        grad_here(chunk).start()

    @pl.when(jnp.logical_not(inner))
    def _():
        for chunk in range(chunks):
            start([wide(chunk, me, partner(k)) for k in hops if k > 1])

    for chunk in range(chunks):
        grad_here(chunk).wait()
        for k in turns:
            grad_copy(chunk, peer(k), mine).wait_recv()
        own(chunk).wait()
        for k in hops:
            wide(chunk, partner(k), me).wait_recv()
        if chunk >= 2:
            finish(stores(chunk - 2))

        def update(p, carry, chunk=chunk):
            j = incoming[p]
            grad = got_grads[0, chunk, p].astype(jnp.float32)
            for r in range(1, replicas):
                grad = grad + got_grads[r, chunk, p].astype(jnp.float32)
            weight_here, first_here, second_here = adam_step(
                decode(got[chunk][0, j]),
                got[chunk][1, j].astype(jnp.float32),
                got[chunk][2, j].astype(jnp.float32),
                grad * (1.0 / replicas),
            )
            rounded[chunk, p] = weight_here.astype(jnp.bfloat16)
            raw[chunk % 2][0, p] = weight_here
            raw[chunk % 2][1, p] = first_here
            raw[chunk % 2][2, p] = second_here
            return carry

        size = slots // parts
        for part in range(parts):
            lax.fori_loop(part * size, (part + 1) * size, update, 0, unroll=math.gcd(size, 8))
            start([last_copy(chunk, part, mine, far(k)) for k in across])
            last_copy(chunk, part, mine, twin).start()
        start(stores(chunk))
        last_here(chunk).start()

    pieces = [(chunk, part) for chunk in range(chunks) for part in range(parts)]
    for chunk, part in pieces:
        for k in across:
            last_copy(chunk, part, far(k), mine).wait_recv()
            relay(chunk, part, far(k)).start()

    for chunk, part in pieces:
        last_copy(chunk, part, twin, mine).wait_recv()
        last_copy(chunk, part, mine, twin).wait_send()
        for k in across:
            last_copy(chunk, part, mine, far(k)).wait_send()
            relay(chunk, part, far(k)).wait_send()
            relay(chunk, part, far_twin(k)).wait_recv()

    for chunk in range(chunks):
        last_here(chunk).wait()
        for k in turns:
            grad_copy(chunk, mine, peer(k)).wait_send()
        for k in hops:
            wide(chunk, me, partner(k)).wait_send()
        if chunk >= chunks - 2:
            finish(stores(chunk))


def exchange(outgoing, incoming, weight, first, second, grads, groups, replicas, capacity):
    slots, rows, lanes = weight.shape
    chunks = rows // ROWS
    length = groups * capacity
    whole = pltpu.VMEM(weight.shape, jnp.float32)
    anywhere = pl.BlockSpec(memory_space=pl.ANY)
    table = pl.BlockSpec(memory_space=pltpu.SMEM)
    dma = pltpu.SemaphoreType.DMA
    parts = PARTS if slots % PARTS == 0 else 1
    block = slots * ROWS * lanes
    scratch = block * (24 + 2 * chunks + 2 * chunks * replicas) + 12 * chunks * length * ROWS * lanes
    return pl.pallas_call(
        functools.partial(exchange_kernel, groups, replicas, capacity, chunks),
        out_shape=(whole, whole, whole, pltpu.VMEM(grads.shape[1:], jnp.bfloat16)),
        in_specs=[table, table] + [anywhere] * 4,
        out_specs=(anywhere,) * 4,
        scratch_shapes=[
            [pltpu.VMEM((3, slots, ROWS, lanes), jnp.float32)] * 2,
            pltpu.VMEM((chunks, 3, length, ROWS, lanes), jnp.bfloat16),
            [pltpu.VMEM((3, length, ROWS, lanes), jnp.bfloat16)] * chunks,
            pltpu.VMEM((replicas, chunks, slots, ROWS, lanes), jnp.bfloat16),
            pltpu.VMEM((chunks, slots, ROWS, lanes), jnp.bfloat16),
            dma((2, 3)),
            dma((2, 3)),
            dma((chunks,)),
            dma((chunks, groups)),
            dma((chunks, groups)),
            dma((chunks,)),
            dma((chunks, replicas)),
            dma((chunks, replicas)),
            dma((chunks,)),
            dma((chunks, parts, replicas)),
            dma((chunks, parts, replicas)),
            dma((chunks, parts, replicas)),
        ],
        compiler_params=pltpu.CompilerParams(
            collective_id=0, has_side_effects=True, vmem_limit_bytes=scratch + SPARE
        ),
        name="exchange",
    )(outgoing, incoming, weight, first, second, grads)


def shards(master_weight, first_moment, second_moment, grads, dest_table):
    groups = lax.axis_size("tensor")
    rank_here = lax.axis_index("tensor")
    slots = master_weight.shape[0]
    capacity = 2 * ((slots + 2 * groups - 1) // (2 * groups))
    outgoing, incoming = routes(dest_table, slots, groups, capacity, rank_here)
    replicas = lax.axis_size("dp")
    return exchange(
        outgoing, incoming, master_weight, first_moment, second_moment, grads,
        groups, replicas, capacity,
    )


def solution(mesh):
    placed = (
        P(("section", "tensor"), "dp", None),
        P(("section", "tensor"), "dp", None),
        P(("section", "tensor"), "dp", None),
        P("dp", ("section", "tensor"), None, None),
        P(),
    )
    return jax.shard_map(
        shards,
        mesh=mesh,
        in_specs=placed,
        out_specs=(
            P(("section", "tensor"), "dp", None),
            P(("section", "tensor"), "dp", None),
            P(("section", "tensor"), "dp", None),
            P(("section", "tensor"), None, None),
        ),
        check_vma=False,
    )
```
